128 devices in a mesh: ctx: 16 (over x, z), head: 8 (over y, core).
Axes of the slice: x: 4, y: 4, z: 4, core: 2. Of those that a mesh axis runs over, the one named last changes fastest.
Arguments:
- xbc: bfloat16 [16384, 18432], P(('ctx', 'head')), may hold values from -6 to 6
- dt_raw: bfloat16 [16384, 256], P(('ctx', 'head')), may hold values from -8 to 0
- decay_rate: float32 [256], P('head'), may hold values from 0.001 to 0.3
- skip: float32 [256], P('head'), may hold values from 0.5 to 1.5
- conv_w: bfloat16 [4, 18432], P(None, 'head'), may hold values from -3 to 3
- conv_b: bfloat16 [18432], P('head'), may hold values from -3 to 3
- gain: bfloat16 [16384], P('head'), may hold values from 0.5 to 1.5
- starts: int32 [16], replicated, may hold values from 0 to 1024, as said below
- assign: int32 [4], replicated, may hold values from 0 to 15, as said below
Outputs:
- mixed: bfloat16 [16384, 16384], P(('ctx', 'head'))
- decode_states: float32 [16, 256, 64, 128], P('ctx', 'head')
- decode_tails: bfloat16 [16, 3, 18432], P('ctx', None, 'head')
The draws below stay inside these ranges and needn't reach their ends.
Inputs may be any that keep to these rules, and one draw needn't show every extreme that they name: starts[0] = 0; exactly 4 entries are below 1024, each a multiple of 512; the others equal 1024. `assign`: the 4 entries are distinct.
All inputs are finite; a program needn't handle non-finite values.
Results may differ from the reference program's by a relative error of at most 0.0036.
Values may be sent and summed in bfloat16 or wider, within the bound.
No kernel may reach another device: no remote copies, remote signals or barrier semaphores. Data moves between devices by JAX's collectives and lax.ppermute only.
A program may use at most 128 MiB of HBM per device.

```python
import math
from functools import partial
import jax
import jax.numpy as jnp
from jax import lax

HEADS = 256
HEAD_DIM = 64
STATE = 128
GROUPS = 8
CONV = 4
BLOCK = 512
PROMPTS = 4
TOK_DEV = 1024
TOKENS = 16384
CONV_CH = 18432


def shared_heads(key):
    key = jax.random.fold_in(key, 7031)
    keys = jax.random.split(key, 5)
    share = 0.5
    quick_heads = jax.random.uniform(keys[0], (HEADS,)) < share
    total_decay = jnp.exp(jax.random.uniform(keys[1], (HEADS,), minval=math.log(0.3), maxval=math.log(1.5)))
    quick_rate = jnp.exp(jax.random.uniform(keys[2], (HEADS,), minval=math.log(0.15), maxval=math.log(0.3)))
    slow_step = 1.0 / math.sqrt(TOKENS)
    rate = jnp.where(quick_heads, quick_rate, total_decay / (TOKENS * slow_step))
    base = jnp.where(quick_heads, 0.15, slow_step)
    return (rate, base, keys[3], keys[4])


def draw_decay_rate(key, part):
    rate, base, key_slab, key_row = shared_heads(key)
    return rate.astype(jnp.float32)


def draw_dt_raw(key, part):
    rate, base, key_slab, key_row = shared_heads(key)
    slices = TOKENS // TOK_DEV
    slab_factor = jnp.exp(jax.random.uniform(key_slab, (slices, 1, HEADS), minval=math.log(0.5), maxval=math.log(2.0)))
    row_factor = jnp.exp(jax.random.uniform(key_row, (slices, TOK_DEV, HEADS), minval=math.log(0.7), maxval=math.log(1.4)))
    step_size = (base[None, None, :] * slab_factor * row_factor).reshape(TOKENS, HEADS)
    return jnp.log(jnp.expm1(step_size)).astype(jnp.bfloat16)


def draw_starts(key, part):
    key = jax.random.fold_in(key, 4421)
    key_order, key_offset = jax.random.split(key)
    slices = TOKENS // TOK_DEV
    chosen = jax.random.permutation(key_order, slices - 1)[:PROMPTS - 1] + 1
    offsets = jax.random.randint(key_offset, (PROMPTS - 1,), 0, TOK_DEV // BLOCK) * BLOCK
    result = jnp.full((slices,), TOK_DEV, jnp.int32).at[0].set(0)
    return result.at[chosen].set(offsets.astype(jnp.int32)).astype(jnp.int32)


def draw_assign(key, part):
    key = jax.random.fold_in(key, 9157)
    key_pick, key_order = jax.random.split(key)
    slices = TOKENS // TOK_DEV
    others = jax.random.permutation(key_pick, slices - 2)[:PROMPTS - 2] + 1
    chosen = jnp.concatenate([jnp.array([0, slices - 1], jnp.int32), others.astype(jnp.int32)])
    return chosen[jax.random.permutation(key_order, PROMPTS)].astype(jnp.int32)


def level_of(own_key, dims, cuts, least, high):
    level = 1.0
    for axis_at, shards_of in cuts:
        steps = jax.random.uniform(jax.random.fold_in(jax.random.fold_in(own_key, 6), axis_at), (shards_of,), jnp.float32, least / len(cuts), high / len(cuts))
        level = level * jnp.repeat(jnp.exp(steps), dims[axis_at] // shards_of).reshape((-1,) + (1,) * (len(dims) - 1 - axis_at))
    return level


def noise(key, shape, width, bound, cuts=(), kind=jnp.bfloat16):
    entries = jax.random.normal(key, shape, jnp.float32) * width
    if len(cuts) > 0:
        entries = level_of(key, shape, cuts, -0.22, 0.18) * entries
    return jnp.clip(entries, min=-bound, max=bound).astype(kind)


def setup_inputs(seed: int = 0) -> dict:
    key_list = jax.random.split(jax.random.key(seed), 10)
    xbc = noise(key_list[0], (TOKENS, CONV_CH), 1.0, 6.0, ((0, 128),))
    dt_raw = draw_dt_raw(jax.random.fold_in(key_list[9], 71), 0)
    decay_rate = draw_decay_rate(jax.random.fold_in(key_list[9], 71), 0)
    skip = jnp.clip(0.5 + 1.0 * jax.random.uniform(key_list[3], (HEADS,), jnp.float32) ** level_of(key_list[3], (HEADS,), ((0, 8),), -0.2, 0.2), 0.5, 1.5)
    conv_w = noise(key_list[4], (CONV, CONV_CH), CONV ** -0.5, 3.0, ((1, 8),))
    conv_b = noise(key_list[5], (CONV_CH,), 0.5, 3.0, ((0, 8),))
    gain = jnp.clip(1.0 + 0.1 * jax.random.normal(key_list[6], (HEADS * HEAD_DIM,), jnp.float32), 0.5, 1.5).astype(jnp.bfloat16)
    starts = draw_starts(jax.random.fold_in(key_list[9], 71), 0)
    assign = draw_assign(jax.random.fold_in(key_list[9], 71), 0)
    return {"xbc": xbc, "dt_raw": dt_raw, "decay_rate": decay_rate, "skip": skip, "conv_w": conv_w, "conv_b": conv_b, "gain": gain, "starts": starts, "assign": assign}


def conv_slice(conv_w, conv_b, slice_item):
    raw_rows, prev_rows, begin = slice_item
    conv_lag = CONV - 1
    extended = jnp.concatenate([prev_rows, raw_rows], 0)
    local_rows = jnp.arange(TOK_DEV, dtype=jnp.int32)
    summed = jnp.zeros(raw_rows.shape, jnp.float32) + conv_b.astype(jnp.float32)[None, :]
    for tap_idx in range(CONV):
        usable = (local_rows - conv_lag + tap_idx >= begin) | (local_rows < begin)
        term = extended[tap_idx:tap_idx + TOK_DEV].astype(jnp.float32) * conv_w[tap_idx].astype(jnp.float32)[None, :]
        summed = summed + jnp.where(usable[:, None], term, 0.0)
    return jax.nn.silu(summed).astype(jnp.bfloat16)

def rounded(array):
    return lax.optimization_barrier(array.astype(jnp.bfloat16)).astype(jnp.float32)

def reference(xbc, dt_raw, decay_rate, skip, conv_w, conv_b, gain, starts, assign):
    conv_lag = CONV - 1
    slices = TOKENS // TOK_DEV
    per_group = HEADS // GROUPS
    width_x = per_group * HEAD_DIM
    group_w = width_x + 2 * STATE
    blocks_all = TOKENS // BLOCK
    blocks_per = TOK_DEV // BLOCK
    starts = starts.astype(jnp.int32)
    raw_slices = xbc.reshape(slices, TOK_DEV, CONV_CH)
    prev_all = jnp.concatenate([jnp.zeros((1, conv_lag, CONV_CH), xbc.dtype), raw_slices[:-1, TOK_DEV - conv_lag:]], 0)
    act = lax.map(partial(conv_slice, conv_w, conv_b), (raw_slices, prev_all, starts))
    act = act.reshape(blocks_all, BLOCK, GROUPS, group_w)
    steps_raw = dt_raw.reshape(blocks_all, BLOCK, HEADS)
    block_ids = jnp.arange(blocks_all, dtype=jnp.int32)
    opens = starts[block_ids // blocks_per] == block_ids % blocks_per * BLOCK
    positions = jnp.arange(BLOCK, dtype=jnp.int32)
    causal = positions[:, None] >= positions[None, :]
    rates = decay_rate.astype(jnp.float32).reshape(GROUPS, per_group)
    skips = skip.astype(jnp.float32).reshape(GROUPS, per_group)
    gains = gain.astype(jnp.float32).reshape(GROUPS, width_x)

    def block_step(carry, block_item):
        carried, finals, count = carry
        block_act, block_raw, opening = block_item
        record = opening & (count >= 1)
        slot_hit = (jnp.arange(PROMPTS, dtype=jnp.int32) == count - 1) & record
        finals = jnp.where(slot_hit[:, None, None, None], carried[None], finals)
        count = count + opening.astype(jnp.int32)
        carried = jnp.where(opening, jnp.zeros_like(carried), carried)
        values_f = block_act[:, :, :width_x].reshape(BLOCK, GROUPS, per_group, HEAD_DIM).astype(jnp.float32)
        b_in = block_act[:, :, width_x:width_x + STATE].astype(jnp.float32)
        c_out = block_act[:, :, width_x + STATE:].astype(jnp.float32)
        step_sizes = jax.nn.softplus(block_raw.astype(jnp.float32)).reshape(BLOCK, GROUPS, per_group)
        cumulative = jnp.cumsum(-step_sizes * rates[None], 0)
        scores = jnp.einsum('tgn,sgn->gts', c_out, b_in)
        cum_heads = cumulative.transpose(1, 2, 0)
        log_gap = cum_heads[:, :, :, None] - cum_heads[:, :, None, :]
        weights = jnp.where(causal, jnp.exp(jnp.where(causal, log_gap, 0.0)), 0.0)
        weights = weights * scores[:, None] * step_sizes.transpose(1, 2, 0)[:, :, None, :]
        inner = jnp.einsum('gkts,sgkp->tgkp', rounded(weights), values_f)
        held = rounded(carried).reshape(GROUPS, per_group, HEAD_DIM, STATE)
        from_state = jnp.exp(cumulative)[..., None] * jnp.einsum('tgn,gkpn->tgkp', c_out, held)
        end_weight = jnp.exp(cumulative[-1][None] - cumulative) * step_sizes
        weighted = rounded(values_f * end_weight[..., None])
        fresh = jnp.einsum('sgkp,sgn->gkpn', weighted, b_in).reshape(HEADS, HEAD_DIM, STATE)
        carried = jnp.exp(cumulative[-1]).reshape(HEADS)[:, None, None] * carried + fresh
        total = inner + from_state + skips[None, :, :, None] * values_f
        flat = total.reshape(BLOCK, GROUPS, width_x)
        mean_sq = lax.optimization_barrier(jnp.mean(flat * flat, -1, keepdims=True))
        normed = flat * lax.rsqrt(mean_sq + 1e-05) * gains[None]
        return ((carried, finals, count), normed.reshape(BLOCK, HEADS * HEAD_DIM).astype(jnp.bfloat16))
    init = (jnp.zeros((HEADS, HEAD_DIM, STATE), jnp.float32), jnp.zeros((PROMPTS, HEADS, HEAD_DIM, STATE), jnp.float32), jnp.zeros((), jnp.int32))
    (last_state, finals, count), mixed = lax.scan(block_step, init, (act, steps_raw, opens))
    prompt_ids = jnp.arange(PROMPTS, dtype=jnp.int32)
    finals = jnp.where((prompt_ids == PROMPTS - 1)[:, None, None, None], last_state[None], finals)
    mixed = mixed.reshape(TOKENS, HEADS * HEAD_DIM)
    valid = starts < TOK_DEV
    rank = (jnp.cumsum(valid.astype(jnp.int32)) - 1).astype(jnp.int32)
    anchor = (jnp.arange(slices, dtype=jnp.int32) * TOK_DEV + starts).astype(jnp.int32)
    picked = valid[None, :] & (rank[None, :] == prompt_ids[:, None] + 1)
    ends = lax.optimization_barrier(jnp.sum(jnp.where(picked, anchor[None, :], 0), 1)).astype(jnp.int32)
    ends = (ends + jnp.where(prompt_ids == PROMPTS - 1, TOKENS, 0)).astype(jnp.int32)
    row_ids = jnp.arange(slices, dtype=jnp.int32)
    decode_states = jnp.zeros((slices, HEADS, HEAD_DIM, STATE), jnp.float32)
    decode_tails = jnp.zeros((slices, conv_lag, CONV_CH), jnp.bfloat16)
    for prompt in range(PROMPTS):
        target = row_ids == assign[prompt]
        decode_states = jnp.where(target[:, None, None, None], finals[prompt][None], decode_states)
        tail_rows = lax.dynamic_slice_in_dim(xbc, (ends[prompt] - conv_lag).astype(jnp.int32), conv_lag, 0)
        decode_tails = jnp.where(target[:, None, None], tail_rows[None], decode_tails)
    return (mixed, decode_states, decode_tails)
```

```python
import functools

import jax
import jax.numpy as jnp
from jax import lax
from jax.experimental import pallas as pl
from jax.experimental.pallas import tpu as pltpu
from jax.sharding import Mesh, PartitionSpec as P

HEAD_DIM = 64
STATE = 128
GROUPS = 8
PER_GROUP = 32
WIDTH_X = PER_GROUP * HEAD_DIM
GROUP_W = WIDTH_X + 2 * STATE
LOC = GROUPS // 2
ROWS = 128
CHUNK = 2 * ROWS
CHIPS = 64
OWNERS = 16
PAY = 136
CONV = 4
LAG = CONV - 1

F32 = jnp.float32
BF16 = jnp.bfloat16


def dot(a, b, ca=1, cb=0):
    return lax.dot_general(a, b, (((ca,), (cb,)), ((), ())), preferred_element_type=F32)


def split2(v):
    hi = v.astype(BF16)
    return hi, (v - hi.astype(F32)).astype(BF16)


def spread(g):
    head = lax.broadcasted_iota(jnp.int32, (128, WIDTH_X), 0)
    col = lax.broadcasted_iota(jnp.int32, (128, WIDTH_X), 1)
    return (head == g * PER_GROUP + col // HEAD_DIM).astype(BF16)


def first_kernel(ids, starts, mine, recv, halo_a, halo_b, dt_mine, dt_recv, wts, wall,
                 pay, act, xb, score, scale, ext, bexp, bpart, lrow):
    g = pl.program_id(0)
    core = ids[0]

    @pl.when(g == 0)
    def _():
        dm, dr = dt_mine[...].astype(F32), dt_recv[...].astype(F32)
        own_first = core == 0
        raw = jnp.concatenate([jnp.where(own_first, dm, dr), jnp.where(own_first, dr, dm)], 0)
        step = jnp.log1p(jnp.exp(raw))
        decay = wall[0, 6:7, 0:128] + wall[1, 6:7, 0:128] + wall[2, 6:7, 0:128] + wall[3, 6:7, 0:128]
        cum = -step * decay
        row = lax.broadcasted_iota(jnp.int32, (CHUNK, 128), 0)
        shift = 1
        while shift < CHUNK:
            cum = cum + jnp.where(row >= shift, pltpu.roll(cum, shift, 0), 0.0)
            shift *= 2
        ahi, alo = split2(jnp.exp(cum))
        scale[0] = ahi
        scale[1] = alo
        bhi, blo = split2(jnp.exp(-cum) * step)
        bpart[0] = bhi
        bpart[1] = blo
        last = cum[CHUNK - 8 :, :]
        hi = last.astype(BF16)
        rest = last - hi.astype(F32)
        mid = rest.astype(BF16)
        low = (rest - mid.astype(F32)).astype(BF16)
        lrow[0:1] = hi.astype(F32)[7:8]
        lrow[1:2] = mid.astype(F32)[7:8]
        lrow[2:3] = low.astype(F32)[7:8]
        lrow[3:8] = jnp.zeros((5, 128), F32)

    m, r = mine[...].astype(F32), recv[...].astype(F32)
    ext[8 : 8 + ROWS, :] = jnp.where(core == 0, m, r)
    ext[8 + ROWS : 8 + CHUNK, :] = jnp.where(core == 0, r, m)
    opens = starts[ids[2]] == ids[1] * CHUNK
    halo = halo_a[...].astype(F32) + halo_b[...].astype(F32)
    ext[8 - LAG : 8, :] = jnp.where(opens, jnp.zeros_like(halo), halo)

    one_hot = spread(g)
    bexp[...] = dot(bpart[0], one_hot) + dot(bpart[1], one_hot)

    def conv(at):
        total = wts[0, CONV : CONV + 1, at] + jnp.zeros((CHUNK, 128), F32)
        for tap in range(CONV):
            total = total + ext[8 - LAG + tap : 8 - LAG + tap + CHUNK, at] * wts[0, tap : tap + 1, at]
        return (total * jax.nn.sigmoid(total)).astype(BF16)

    def strip(j, _):
        at = pl.ds(pl.multiple_of(j * 128, 128), 128)
        val = conv(at)
        act[:, at] = val
        xb[:, at] = (val.astype(F32) * bexp[:, at]).astype(BF16)
        return 0

    lax.fori_loop(0, WIDTH_X // 128, strip, 0)
    b_in = conv(pl.ds(WIDTH_X, 128))
    c_out = conv(pl.ds(WIDTH_X + STATE, 128))
    act[:, WIDTH_X : WIDTH_X + STATE] = b_in
    act[:, WIDTH_X + STATE :] = c_out
    s = dot(c_out, b_in, 1, 1)
    t_at = lax.broadcasted_iota(jnp.int32, (CHUNK, CHUNK), 0)
    s_at = lax.broadcasted_iota(jnp.int32, (CHUNK, CHUNK), 1)
    score[...] = jnp.where(s_at <= t_at, s, 0.0).astype(BF16)

    tail = ext[CHUNK : 8 + CHUNK, :]
    extra_low = lrow[...]
    for o in range(OWNERS):
        fresh = dot(b_in, xb[:, o * 128 : (o + 1) * 128], 0, 0)
        pay[0, o, 0:STATE, :] = fresh.astype(BF16)
        rows = []
        for slot in range(4):
            piece = o * 4 + slot
            tap, block = divmod(piece, GROUP_W // 128)
            if tap < LAG:
                rows.append(tail[8 - LAG + tap : 9 - LAG + tap, block * 128 : (block + 1) * 128])
            else:
                rows.append(jnp.zeros((1, 128), F32))
        pay[0, o, STATE:PAY, :] = jnp.concatenate(rows + [extra_low[0:4]], 0).astype(BF16)


def inner_kernel(score, xb, act, scale, wall, part):
    g = pl.program_id(0)
    one_hot = spread(g)
    skip = wall[0, 6:7, 128:256] + wall[1, 6:7, 128:256] + wall[2, 6:7, 128:256] + wall[3, 6:7, 128:256]
    shi = skip.astype(BF16)
    rest = skip - shi.astype(F32)
    smid = rest.astype(BF16)
    slo = (rest - smid.astype(F32)).astype(BF16)
    s = score[...]
    for j in range(0, WIDTH_X, 256):
        at = slice(j, j + 256)
        e = one_hot[:, at]
        spread_skip = sum(dot(jnp.broadcast_to(v, (8, 128)), e) for v in (shi, smid, slo))[0:1]
        spread_a = dot(scale[0], e) + dot(scale[1], e)
        part[:, at] = spread_a * dot(s, xb[:, at]) + spread_skip * act[:, at].astype(F32)


def scan_kernel(ids, starts, assign, got, held, fin, dec):
    lane = lax.broadcasted_iota(jnp.int32, (CHIPS, 128), 1)
    total = (got[:, STATE + 4, :].astype(F32) + got[:, STATE + 5, :].astype(F32)
             + got[:, STATE + 6, :].astype(F32))
    head = ids[1] * PER_GROUP + ids[2] * 2
    d0 = jnp.sum(jnp.where(lane == head, total, 0.0), 1, keepdims=True)
    d1 = jnp.sum(jnp.where(lane == head + 1, total, 0.0), 1, keepdims=True)
    dec[...] = jnp.exp(jnp.where(lane < HEAD_DIM, d0, d1))
    fin[...] = jnp.zeros_like(fin)

    def step(p, carry):
        state, count = carry
        ctx, y = p // 4, p % 4
        at = y * OWNERS + ctx
        opens = starts[ctx] == y * CHUNK
        state = jnp.where(opens, 0.0, state)
        count = count + opens.astype(jnp.int32)
        held[at] = state.astype(BF16)
        state = dec[pl.ds(at, 1), :] * (state + got[at, 0:STATE, :].astype(F32))
        nxt = jnp.minimum(p + 1, CHIPS - 1)
        ends = (p == CHIPS - 1) | (starts[nxt // 4] == (nxt % 4) * CHUNK)

        @pl.when(ends)
        def _():
            to = assign[count - 1]
            fin[to, 0:STATE, :] = state.T.astype(BF16)
            fin[to, STATE:PAY, :] = got[at, STATE:PAY, :]

        return state, count

    lax.fori_loop(0, CHIPS, step, (jnp.zeros((STATE, 128), F32), jnp.int32(0)))


def last_kernel(ids, part, act_c, scale, held, wts, out, send, y):
    g = pl.program_id(0)
    one_hot = spread(g)
    c = act_c[...]
    square = jnp.zeros((CHUNK, 128), F32)
    for o in range(0, OWNERS, 2):
        at = slice(o * 128, (o + 2) * 128)
        e = one_hot[:, at]
        h = jnp.concatenate([held[0, o], held[0, o + 1]], 1)
        total = part[:, at] + (dot(scale[0], e) + dot(scale[1], e)) * dot(c, h)
        y[:, at] = total
        square = square + total[:, :128] * total[:, :128] + total[:, 128:] * total[:, 128:]
    mean = jnp.sum(square, 1, keepdims=True) * (1.0 / WIDTH_X)
    y[:, WIDTH_X:] = jnp.broadcast_to(lax.rsqrt(mean + 1e-05), (CHUNK, 128))
    core = ids[0]
    for ref, half in ((out, core), (send, 1 - core)):
        rows = pl.ds(pl.multiple_of(half * ROWS, ROWS), ROWS)
        inv = y[rows, WIDTH_X:]
        for j in range(0, WIDTH_X, 128):
            at = slice(j, j + 128)
            ref[:, at] = (y[rows, at] * inv * wts[0, CONV + 1 : CONV + 2, at]).astype(BF16)


def place_kernel(ids, whole, recv, out):
    out[...] = recv[...]


def params(**kw):
    return pltpu.CompilerParams(dimension_semantics=("arbitrary",), **kw)


def other_groups(array, width, which):
    parts = [
        lax.dynamic_slice_in_dim(array, (2 * i + which) * width, width, 1) for i in range(LOC)
    ]
    return parts


def shards(xbc, dt_raw, decay_rate, skip, conv_w, conv_b, gain, starts, assign):
    core = lax.axis_index("core").astype(jnp.int32)
    y_at = lax.axis_index("y").astype(jnp.int32)
    ctx = (lax.axis_index("x") * 4 + lax.axis_index("z")).astype(jnp.int32)
    at = jnp.arange(4, dtype=jnp.int32)
    ids = jnp.where(at == 0, core, jnp.where(at == 1, y_at, ctx))

    swap = [(0, 1), (1, 0)]
    outgoing = jnp.concatenate(
        other_groups(xbc, GROUP_W, 1 - core) + other_groups(dt_raw, PER_GROUP, 1 - core), 1
    )
    recv = lax.ppermute(outgoing, "core", swap)
    dt_mine = jnp.concatenate(other_groups(dt_raw, PER_GROUP, core), 1)

    names = ("x", "z", "y", "core")
    rim = xbc[ROWS - LAG :]
    rims = [
        jnp.concatenate([rim[:, (2 * i + k) * GROUP_W : (2 * i + k + 1) * GROUP_W] for i in range(LOC)], 1)
        for k in range(2)
    ]
    halos = [
        lax.ppermute(rims[k], names, [(2 * p + 1, 2 * p + 2 + k) for p in range(CHIPS - 1)])
        for k in range(2)
    ]

    lanes = jnp.arange(128, dtype=jnp.int32) // PER_GROUP == y_at
    small = jnp.concatenate(
        [jnp.where(lanes, jnp.tile(decay_rate, 4), 0.0), jnp.where(lanes, jnp.tile(skip, 4), 0.0)]
    )
    table = jnp.concatenate(
        [
            conv_w.astype(F32),
            conv_b.astype(F32)[None],
            jnp.pad(gain.astype(F32), (0, GROUP_W - WIDTH_X))[None],
            jnp.pad(small, (0, GROUP_W - 256))[None],
            jnp.zeros((1, GROUP_W), F32),
        ],
        0,
    )
    wall = lax.all_to_all(jnp.broadcast_to(table[None], (4, 8, GROUP_W)), "y", 0, 0, tiled=True)

    whole_wall = pl.BlockSpec((4, 8, GROUP_W), lambda g, *_: (0, 0, 0))
    group_wall = pl.BlockSpec((1, 8, GROUP_W), lambda g, *_: (g, 0, 0))
    scale_spec = pl.BlockSpec((2, CHUNK, 128), lambda g, *_: (0, 0, 0))
    wide = lambda n: pl.BlockSpec((CHUNK, n), lambda g, *_: (0, g))

    pay, act, xb, score, scale = pl.pallas_call(
        first_kernel,
        name="first",
        grid_spec=pltpu.PrefetchScalarGridSpec(
            num_scalar_prefetch=2,
            grid=(LOC,),
            in_specs=[
                pl.BlockSpec((ROWS, GROUP_W), lambda g, ids, st: (0, 2 * g + ids[0])),
                pl.BlockSpec((ROWS, GROUP_W), lambda g, ids, st: (0, g)),
                pl.BlockSpec((LAG, GROUP_W), lambda g, ids, st: (0, g)),
                pl.BlockSpec((LAG, GROUP_W), lambda g, ids, st: (0, g)),
                pl.BlockSpec((ROWS, 128), lambda g, ids, st: (0, 0)),
                pl.BlockSpec((ROWS, 128), lambda g, ids, st: (0, LOC * GROUP_W // 128)),
                group_wall,
                whole_wall,
            ],
            out_specs=[
                pl.BlockSpec((1, OWNERS, PAY, 128), lambda g, *_: (g, 0, 0, 0)),
                wide(GROUP_W),
                wide(WIDTH_X),
                wide(CHUNK),
                scale_spec,
            ],
            scratch_shapes=[
                pltpu.VMEM((8 + CHUNK, GROUP_W), F32),
                pltpu.VMEM((CHUNK, WIDTH_X), F32),
                pltpu.VMEM((2, CHUNK, 128), BF16),
                pltpu.VMEM((8, 128), F32),
            ],
        ),
        out_shape=[
            jax.ShapeDtypeStruct((LOC, OWNERS, PAY, 128), BF16),
            jax.ShapeDtypeStruct((CHUNK, LOC * GROUP_W), BF16),
            jax.ShapeDtypeStruct((CHUNK, LOC * WIDTH_X), BF16),
            jax.ShapeDtypeStruct((CHUNK, LOC * CHUNK), BF16),
            jax.ShapeDtypeStruct((2, CHUNK, 128), BF16),
        ],
        compiler_params=params(),
        cost_estimate=pl.CostEstimate(flops=2 * 10**9, bytes_accessed=18 * 10**6, transcendentals=0),
    )(ids, starts, xbc, recv, halos[0], halos[1], dt_mine, recv, wall, wall)

    got = lax.all_to_all(pay.reshape(CHIPS, PAY, 128), ("y", "x", "z"), 0, 0, tiled=True)

    part = pl.pallas_call(
        inner_kernel,
        name="inner",
        grid=(LOC,),
        in_specs=[wide(CHUNK), wide(WIDTH_X), wide(GROUP_W), scale_spec, whole_wall],
        out_specs=wide(WIDTH_X),
        out_shape=jax.ShapeDtypeStruct((CHUNK, LOC * WIDTH_X), F32),
        compiler_params=params(),
        cost_estimate=pl.CostEstimate(flops=2 * 10**9, bytes_accessed=20 * 10**6, transcendentals=0),
    )(score, xb, act, scale, wall)

    smem = pl.BlockSpec(memory_space=pltpu.SMEM)
    vmem = pl.BlockSpec(memory_space=pltpu.VMEM)
    held, fin = pl.pallas_call(
        scan_kernel,
        name="scan",
        in_specs=[smem, smem, smem, vmem],
        out_specs=[vmem, vmem],
        out_shape=[
            jax.ShapeDtypeStruct((CHIPS, STATE, 128), BF16),
            jax.ShapeDtypeStruct((OWNERS, PAY, 128), BF16),
        ],
        scratch_shapes=[pltpu.VMEM((CHIPS, 128), F32)],
        cost_estimate=pl.CostEstimate(flops=10**7, bytes_accessed=5 * 10**6, transcendentals=0),
    )(ids, starts, assign, got)

    back = lax.all_to_all(held, ("y", "x", "z"), 0, 0, tiled=True)
    ready, fin = lax.optimization_barrier((back, fin))
    rows_got = lax.all_to_all(fin, ("x", "z"), 0, 0, tiled=True)

    out, send = pl.pallas_call(
        last_kernel,
        name="last",
        grid_spec=pltpu.PrefetchScalarGridSpec(
            num_scalar_prefetch=1,
            grid=(LOC,),
            in_specs=[
                wide(WIDTH_X),
                pl.BlockSpec((CHUNK, STATE), lambda g, ids: (0, GROUP_W // 128 * (g + 1) - 1)),
                scale_spec,
                pl.BlockSpec((1, OWNERS, STATE, 128), lambda g, ids: (g, 0, 0, 0)),
                group_wall,
            ],
            out_specs=[
                pl.BlockSpec((ROWS, WIDTH_X), lambda g, ids: (0, 2 * g + ids[0])),
                pl.BlockSpec((ROWS, WIDTH_X), lambda g, ids: (0, g)),
            ],
            scratch_shapes=[pltpu.VMEM((CHUNK, WIDTH_X + 128), F32)],
        ),
        out_shape=[
            jax.ShapeDtypeStruct((ROWS, GROUPS * WIDTH_X), BF16),
            jax.ShapeDtypeStruct((ROWS, LOC * WIDTH_X), BF16),
        ],
        compiler_params=params(),
        cost_estimate=pl.CostEstimate(flops=10**9, bytes_accessed=15 * 10**6, transcendentals=0),
    )(ids, part, act, scale, ready.reshape(LOC, OWNERS, STATE, 128), wall)

    theirs = lax.ppermute(send, "core", swap)
    mixed = pl.pallas_call(
        place_kernel,
        name="place",
        grid_spec=pltpu.PrefetchScalarGridSpec(
            num_scalar_prefetch=1,
            grid=(LOC,),
            in_specs=[
                pl.BlockSpec(memory_space=pl.ANY),
                pl.BlockSpec((ROWS, WIDTH_X), lambda g, ids: (0, g)),
            ],
            out_specs=pl.BlockSpec((ROWS, WIDTH_X), lambda g, ids: (0, 2 * g + 1 - ids[0])),
        ),
        out_shape=jax.ShapeDtypeStruct((ROWS, GROUPS * WIDTH_X), BF16),
        input_output_aliases={1: 0},
        compiler_params=params(),
    )(ids, out, theirs)

    states = rows_got[:, 0:STATE, :].astype(F32).reshape(1, PER_GROUP, HEAD_DIM, STATE)
    tails = rows_got[:, STATE : STATE + 4, :].reshape(64, 128)[: LAG * GROUP_W // 128]
    return (mixed, states, tails.reshape(1, LAG, GROUP_W))


def solution(mesh):
    axes = ("x", "z", "y", "core")
    fine = Mesh(mesh.devices.reshape(4, 4, 4, 2), axes)
    head = ("y", "core")
    in_specs = (
        P(axes, None),
        P(axes, None),
        P(head),
        P(head),
        P(None, head),
        P(head),
        P(head),
        P(),
        P(),
    )
    out_specs = (P(axes, None), P(("x", "z"), head, None, None), P(("x", "z"), None, head))
    return jax.shard_map(shards, mesh=fine, in_specs=in_specs, out_specs=out_specs, check_vma=False)
```

```python
import jax
import jax.numpy as jnp
from jax import lax
from jax.experimental import pallas as pl
from jax.experimental.pallas import tpu as pltpu
from jax.sharding import Mesh, PartitionSpec as P


HEAD_DIM = 64
STATE = 128
GROUPS = 8
PER_GROUP = 32
WIDTH_X = PER_GROUP * HEAD_DIM
GROUP_W = WIDTH_X + 2 * STATE
LOC = GROUPS // 2
ROWS = 128
CHUNK = 2 * ROWS
CHIPS = 64
OWNERS = 16
PAY = 136
CONV = 4
LAG = CONV - 1

F32 = jnp.float32
BF16 = jnp.bfloat16


def dot(a, b, ca=1, cb=0):
    return lax.dot_general(a, b, (((ca,), (cb,)), ((), ())), preferred_element_type=F32)


def pack3(v):
    lane = lax.broadcasted_iota(jnp.int32, v.shape, 1)
    hi = v.astype(BF16).astype(F32)
    mid = (v - hi).astype(BF16).astype(F32)
    low = (v - hi - mid).astype(BF16).astype(F32)
    three = jnp.where(lane < 32, hi, jnp.where(lane < 64, pltpu.roll(mid, 32, 1), pltpu.roll(low, 64, 1)))
    return jnp.where(lane < 96, three, 0.0).astype(BF16)


def spread():
    row = lax.broadcasted_iota(jnp.int32, (128, WIDTH_X), 0)
    col = lax.broadcasted_iota(jnp.int32, (128, WIDTH_X), 1)
    return ((row & 31) == (col >> 6)).astype(F32).astype(BF16)


def first_kernel(ids, starts, mine, recv, rim_a, rim_b, dt_mine, dt_recv, tab0, tab1, tab2, tab3,
                 pay, act, xb, score, scale, tabs, ext, bexp, one_hot, afull, bfull, lrow, small):
    g = pl.program_id(0)
    core = ids[0]
    own = pl.multiple_of(core * ROWS, ROWS)
    other = pl.multiple_of((1 - core) * ROWS, ROWS)

    @pl.when(g == 0)
    def _():
        col = lax.broadcasted_iota(jnp.int32, (2 * 128, 128), 0)
        lane = lax.broadcasted_iota(jnp.int32, (2 * 128, 128), 1)
        pick = (col == ((2 * (lane >> 5) + core) << 5) + (lane & 31)).astype(F32).astype(BF16)
        afull[pl.ds(own, ROWS), :] = dot(dt_mine[...], pick)
        afull[pl.ds(other, ROWS), :] = dot(dt_recv[...], pick)
        step = jnp.log1p(jnp.exp(afull[...]))
        small[...] = tab0[6:7, 0:256] + tab1[6:7, 0:256] + tab2[6:7, 0:256] + tab3[6:7, 0:256]
        cum = -step * small[:, 0:128]
        row = lax.broadcasted_iota(jnp.int32, (CHUNK, 128), 0)
        shift = 1
        while shift < CHUNK:
            cum = cum + jnp.where(row >= shift, pltpu.roll(cum, shift, 0), 0.0)
            shift *= 2
        afull[...] = jnp.exp(cum)
        bfull[...] = jnp.exp(-cum) * step
        last = cum[CHUNK - 8 :, :]
        hi = last.astype(BF16).astype(F32)
        mid = (last - hi).astype(BF16).astype(F32)
        low = (last - hi - mid).astype(BF16).astype(F32)
        lrow[0:1] = hi[7:8]
        lrow[1:2] = mid[7:8]
        lrow[2:3] = low[7:8]
        lrow[3:8] = jnp.zeros((5, 128), F32)
        one_hot[...] = spread()

    shift = (ids[1] - g) & 3
    table = jnp.where(
        shift == 0, tab0[...], jnp.where(shift == 1, tab1[...], jnp.where(shift == 2, tab2[...], tab3[...]))
    )
    tabs[0] = table
    tabs[0, 7:8, 0:256] = small[...]

    back = (128 - g * PER_GROUP) & 127
    scale[0] = pack3(pltpu.roll(afull[...], back, 1))
    bexp[...] = dot(pack3(pltpu.roll(bfull[...], back, 1)), one_hot[...])
    opens = starts[ids[2]] == ids[1] * CHUNK

    def conv(j):
        at = pl.ds(pl.multiple_of(j * 128, 128), 128)
        halo = rim_a[:, at].astype(F32) + rim_b[:, at].astype(F32)
        ext[j, 8 - LAG : 8, :] = jnp.where(opens, jnp.zeros_like(halo), halo)
        ext[j, pl.ds(8 + own, ROWS), :] = mine[:, at].astype(F32)
        ext[j, pl.ds(8 + other, ROWS), :] = recv[:, at].astype(F32)
        total = tabs[0, CONV : CONV + 1, at] + jnp.zeros((CHUNK, 128), F32)
        for tap in range(CONV):
            total = total + ext[j, 8 - LAG + tap : 8 - LAG + tap + CHUNK, :] * tabs[0, tap : tap + 1, at]
        half = 0.5 * total
        return at, (half * jnp.tanh(half) + half).astype(BF16)

    def strip(j, _):
        at, val = conv(j)
        act[:, at] = val
        xb[:, at] = (val.astype(F32) * bexp[:, at]).astype(BF16)
        return 0

    lax.fori_loop(0, WIDTH_X // 128, strip, 0)
    _, b_in = conv(WIDTH_X // 128)
    _, c_out = conv(WIDTH_X // 128 + 1)
    act[:, WIDTH_X : WIDTH_X + STATE] = b_in
    act[:, WIDTH_X + STATE :] = c_out
    s = dot(c_out, b_in, 1, 1)
    t_at = lax.broadcasted_iota(jnp.int32, (CHUNK, CHUNK), 0)
    s_at = lax.broadcasted_iota(jnp.int32, (CHUNK, CHUNK), 1)
    score[...] = jnp.where(s_at <= t_at, s, 0.0).astype(BF16)

    b_t = b_in.astype(F32).T.astype(BF16)
    for o in range(0, OWNERS, 2):
        fresh = dot(b_t, xb[:, o * 128 : (o + 2) * 128]).astype(BF16)
        pay[0, o, 0:STATE, :] = fresh[:, :128]
        pay[0, o + 1, 0:STATE, :] = fresh[:, 128:]
    for o in range(OWNERS):
        rows = []
        for slot in range(4):
            tap, block = divmod(o * 4 + slot, GROUP_W // 128)
            if tap < LAG:
                end = 8 + CHUNK - LAG + tap
                rows.append(ext[block, end : end + 1, :])
            else:
                rows.append(jnp.zeros((1, 128), F32))
        pay[0, o, STATE:PAY, :] = jnp.concatenate(rows + [lrow[0:4]], 0).astype(BF16)


def inner_kernel(score, xb, act, scale, tabs, part, one_hot):
    @pl.when(pl.program_id(0) == 0)
    def _():
        one_hot[...] = spread()

    back = (128 - pl.program_id(0) * PER_GROUP) & 127
    skip = pack3(pltpu.roll(jnp.broadcast_to(tabs[0, 7:8, 128:256], (8, 128)), back, 1))
    s = score[...]
    for j in range(0, WIDTH_X, 256):
        at = slice(j, j + 256)
        e = one_hot[:, at]
        part[:, at] = dot(scale[0], e) * dot(s, xb[:, at]) + dot(skip, e)[0:1] * act[:, at].astype(F32)


def scan_kernel(ids, starts, assign, got, held, fin, dec):
    lane = lax.broadcasted_iota(jnp.int32, (CHIPS, 128), 1)
    total = (got[:, STATE + 4, :].astype(F32) + got[:, STATE + 5, :].astype(F32)
             + got[:, STATE + 6, :].astype(F32))
    head = ids[1] * PER_GROUP + ids[2] * 2
    d0 = jnp.sum(jnp.where(lane == head, total, 0.0), 1, keepdims=True)
    d1 = jnp.sum(jnp.where(lane == head + 1, total, 0.0), 1, keepdims=True)
    dec[...] = jnp.exp(jnp.where(lane < HEAD_DIM, d0, d1))
    fin[...] = jnp.zeros_like(fin)

    def step(ctx, carry):
        state, count = carry
        for y in range(4):
            at = y * OWNERS + ctx
            opens = starts[ctx] == y * CHUNK
            state = jnp.where(opens, 0.0, state)
            count = count + opens.astype(jnp.int32)
            held[at] = state.astype(BF16)
            state = dec[pl.ds(at, 1), :] * (state + got[at, 0:STATE, :].astype(F32))
            if y < 3:
                ends = starts[ctx] == (y + 1) * CHUNK
            else:
                ends = (ctx == OWNERS - 1) | (starts[jnp.minimum(ctx + 1, OWNERS - 1)] == 0)

            @pl.when(ends)
            def _():
                to = assign[count - 1]
                fin[to, 0:STATE, :] = state.T.astype(BF16)
                fin[to, STATE:PAY, :] = got[at, STATE:PAY, :]

        return state, count

    lax.fori_loop(0, OWNERS, step, (jnp.zeros((STATE, 128), F32), jnp.int32(0)))


def last_kernel(ids, part, act_c, scale, held, tabs, out, y, one_hot):
    @pl.when(pl.program_id(0) == 0)
    def _():
        one_hot[...] = spread()

    c = act_c[...]
    square = jnp.zeros((ROWS, 128), F32)
    for o in range(0, OWNERS, 2):
        at = slice(o * 128, (o + 2) * 128)
        h = jnp.concatenate([held[0, o], held[0, o + 1]], 1)
        total = part[:, at] + dot(scale[0], one_hot[:, at]) * dot(c, h)
        y[:, at] = total
        square = square + total[:, :128] * total[:, :128] + total[:, 128:] * total[:, 128:]
    mean = jnp.sum(square, 1, keepdims=True) * (1.0 / WIDTH_X)
    inv = jnp.broadcast_to(lax.rsqrt(mean + 1e-05), (ROWS, 128))
    for j in range(0, WIDTH_X, 128):
        at = slice(j, j + 128)
        out[:, at] = (y[:, at] * inv * tabs[0, CONV + 1 : CONV + 2, at]).astype(BF16)


def place_kernel(ids, whole, recv, out):
    out[...] = recv[...]


def params():
    return pltpu.CompilerParams(dimension_semantics=("arbitrary",), vmem_limit_bytes=24 * 2**20)


def wide(n):
    return pl.BlockSpec((CHUNK, n), lambda g, *_: (0, g))


TABLE = pl.BlockSpec((1, 8, GROUP_W), lambda g, *_: (g, 0, 0))


def last_call(ids, part, act, scale, held, tabs, own):
    half = (lambda ids: ids[0]) if own else (lambda ids: 1 - ids[0])
    cols = (lambda g, ids: 2 * g + ids[0]) if own else (lambda g, ids: g)
    width = (GROUPS if own else LOC) * WIDTH_X
    return pl.pallas_call(
        last_kernel,
        name="last",
        grid_spec=pltpu.PrefetchScalarGridSpec(
            num_scalar_prefetch=1,
            grid=(LOC,),
            in_specs=[
                pl.BlockSpec((ROWS, WIDTH_X), lambda g, ids: (half(ids), g)),
                pl.BlockSpec((ROWS, STATE), lambda g, ids: (half(ids), GROUP_W // 128 * (g + 1) - 1)),
                pl.BlockSpec((1, ROWS, 128), lambda g, ids: (g, half(ids), 0)),
                pl.BlockSpec((1, OWNERS, STATE, 128), lambda g, ids: (g, 0, 0, 0)),
                TABLE,
            ],
            out_specs=pl.BlockSpec((ROWS, WIDTH_X), lambda g, ids: (0, cols(g, ids))),
            scratch_shapes=[pltpu.VMEM((ROWS, WIDTH_X), F32), pltpu.VMEM((128, WIDTH_X), BF16)],
        ),
        out_shape=jax.ShapeDtypeStruct((ROWS, width), BF16),
        compiler_params=params(),
        cost_estimate=pl.CostEstimate(flops=10**9, bytes_accessed=9 * 10**6, transcendentals=0),
    )(ids, part, act, scale, held, tabs)


def shards(xbc, dt_raw, decay_rate, skip, conv_w, conv_b, gain, starts, assign):
    core = lax.axis_index("core").astype(jnp.int32)
    y_at = lax.axis_index("y").astype(jnp.int32)
    ctx = (lax.axis_index("x") * 4 + lax.axis_index("z")).astype(jnp.int32)
    at = jnp.arange(4, dtype=jnp.int32)
    ids = jnp.where(at == 0, core, jnp.where(at == 1, y_at, ctx))

    swap = [(0, 1), (1, 0)]
    recv = lax.ppermute(xbc, "core", swap)
    dt_recv = lax.ppermute(dt_raw, "core", swap)

    names = ("x", "z", "y", "core")
    rim = xbc[ROWS - LAG :]
    rims = [
        lax.ppermute(rim, names, [(2 * p + 1, 2 * p + 2 + k) for p in range(CHIPS - 1)])
        for k in range(2)
    ]

    lanes = jnp.arange(128, dtype=jnp.int32) // PER_GROUP == y_at
    small = jnp.concatenate(
        [jnp.where(lanes, jnp.tile(decay_rate, 4), 0.0), jnp.where(lanes, jnp.tile(skip, 4), 0.0)]
    )
    table = jnp.concatenate(
        [
            conv_w.astype(F32),
            conv_b.astype(F32)[None],
            jnp.pad(gain.astype(F32), (0, GROUP_W - WIDTH_X))[None],
            jnp.pad(small, (0, GROUP_W - 256))[None],
            jnp.zeros((1, GROUP_W), F32),
        ],
        0,
    )
    tables = [table] + [
        lax.ppermute(table, "y", [(i, (i + s) % 4) for i in range(4)]) for s in range(1, 4)
    ]

    whole_table = pl.BlockSpec((8, GROUP_W), lambda g, *_: (0, 0))
    rows_spec = pl.BlockSpec((ROWS, GROUP_W), lambda g, ids, st: (0, 2 * g + ids[0]))
    rim_spec = pl.BlockSpec((LAG, GROUP_W), lambda g, ids, st: (0, 2 * g + ids[0]))
    dt_spec = pl.BlockSpec((ROWS, 256), lambda g, ids, st: (0, 0))
    scale_spec = pl.BlockSpec((1, CHUNK, 128), lambda g, *_: (g, 0, 0))

    pay, act, xb, score, scale, tabs = pl.pallas_call(
        first_kernel,
        name="first",
        grid_spec=pltpu.PrefetchScalarGridSpec(
            num_scalar_prefetch=2,
            grid=(LOC,),
            in_specs=[rows_spec] * 2 + [rim_spec] * 2 + [dt_spec] * 2 + [whole_table] * 4,
            out_specs=[
                pl.BlockSpec((1, OWNERS, PAY, 128), lambda g, *_: (g, 0, 0, 0)),
                wide(GROUP_W),
                wide(WIDTH_X),
                wide(CHUNK),
                scale_spec,
                TABLE,
            ],
            scratch_shapes=[
                pltpu.VMEM((GROUP_W // 128, 8 + CHUNK, 128), F32),
                pltpu.VMEM((CHUNK, WIDTH_X), F32),
                pltpu.VMEM((128, WIDTH_X), BF16),
                pltpu.VMEM((CHUNK, 128), F32),
                pltpu.VMEM((CHUNK, 128), F32),
                pltpu.VMEM((8, 128), F32),
                pltpu.VMEM((1, 256), F32),
            ],
        ),
        out_shape=[
            jax.ShapeDtypeStruct((LOC, OWNERS, PAY, 128), BF16),
            jax.ShapeDtypeStruct((CHUNK, LOC * GROUP_W), BF16),
            jax.ShapeDtypeStruct((CHUNK, LOC * WIDTH_X), BF16),
            jax.ShapeDtypeStruct((CHUNK, LOC * CHUNK), BF16),
            jax.ShapeDtypeStruct((LOC, CHUNK, 128), BF16),
            jax.ShapeDtypeStruct((LOC, 8, GROUP_W), F32),
        ],
        compiler_params=params(),
        cost_estimate=pl.CostEstimate(flops=2 * 10**9, bytes_accessed=18 * 10**6, transcendentals=0),
    )(ids, starts, xbc, recv, *rims, dt_raw, dt_recv, *tables)

    got = lax.all_to_all(pay.reshape(CHIPS, PAY, 128), ("y", "x", "z"), 0, 0, tiled=True)

    part = pl.pallas_call(
        inner_kernel,
        name="inner",
        grid=(LOC,),
        in_specs=[wide(CHUNK), wide(WIDTH_X), wide(GROUP_W), scale_spec, TABLE],
        out_specs=wide(WIDTH_X),
        out_shape=jax.ShapeDtypeStruct((CHUNK, LOC * WIDTH_X), F32),
        scratch_shapes=[pltpu.VMEM((128, WIDTH_X), BF16)],
        compiler_params=params(),
        cost_estimate=pl.CostEstimate(flops=2 * 10**9, bytes_accessed=20 * 10**6, transcendentals=0),
    )(score, xb, act, scale, tabs)

    smem = pl.BlockSpec(memory_space=pltpu.SMEM)
    vmem = pl.BlockSpec(memory_space=pltpu.VMEM)
    held, fin = pl.pallas_call(
        scan_kernel,
        name="scan",
        in_specs=[smem, smem, smem, vmem],
        out_specs=[vmem, vmem],
        out_shape=[
            jax.ShapeDtypeStruct((CHIPS, STATE, 128), BF16),
            jax.ShapeDtypeStruct((OWNERS, PAY, 128), BF16),
        ],
        scratch_shapes=[pltpu.VMEM((CHIPS, 128), F32)],
        compiler_params=pltpu.CompilerParams(vmem_limit_bytes=24 * 2**20),
        cost_estimate=pl.CostEstimate(flops=10**7, bytes_accessed=5 * 10**6, transcendentals=0),
    )(ids, starts, assign, got)

    back = lax.all_to_all(held, ("y", "x", "z"), 0, 0, tiled=True)
    back, fin = lax.optimization_barrier((back, fin))
    rows_got = lax.all_to_all(fin, ("x", "z"), 0, 0, tiled=True)

    back = back.reshape(LOC, OWNERS, STATE, 128)
    send = last_call(ids, part, act, scale, back, tabs, False)
    theirs = lax.ppermute(send, "core", swap)
    out = last_call(ids, part, act, scale, back, tabs, True)
    mixed = pl.pallas_call(
        place_kernel,
        name="place",
        grid_spec=pltpu.PrefetchScalarGridSpec(
            num_scalar_prefetch=1,
            grid=(LOC,),
            in_specs=[
                pl.BlockSpec(memory_space=pl.ANY),
                pl.BlockSpec((ROWS, WIDTH_X), lambda g, ids: (0, g)),
            ],
            out_specs=pl.BlockSpec((ROWS, WIDTH_X), lambda g, ids: (0, 2 * g + 1 - ids[0])),
        ),
        out_shape=jax.ShapeDtypeStruct((ROWS, GROUPS * WIDTH_X), BF16),
        input_output_aliases={1: 0},
        compiler_params=params(),
    )(ids, out, theirs)

    states = rows_got[:, 0:STATE, :].astype(F32).reshape(1, PER_GROUP, HEAD_DIM, STATE)
    tails = rows_got[:, STATE : STATE + 4, :].reshape(64, 128)[: LAG * GROUP_W // 128]
    return (mixed, states, tails.reshape(1, LAG, GROUP_W))


def solution(mesh):
    axes = ("x", "z", "y", "core")
    fine = Mesh(mesh.devices.reshape(4, 4, 4, 2), axes)
    head = ("y", "core")
    in_specs = (
        P(axes, None),
        P(axes, None),
        P(head),
        P(head),
        P(None, head),
        P(head),
        P(head),
        P(),
        P(),
    )
    out_specs = (P(axes, None), P(("x", "z"), head, None, None), P(("x", "z"), None, head))
    return jax.shard_map(shards, mesh=fine, in_specs=in_specs, out_specs=out_specs, check_vma=False)
```

```python
import jax
import jax.numpy as jnp
from jax import lax
from jax.experimental import pallas as pl
from jax.experimental.pallas import tpu as pltpu
from jax.sharding import Mesh, PartitionSpec as P


HEAD_DIM = 64
STATE = 128
GROUPS = 8
PER_GROUP = 32
WIDTH_X = PER_GROUP * HEAD_DIM
GROUP_W = WIDTH_X + 2 * STATE
LOC = GROUPS // 2
ROWS = 128
CHUNK = 2 * ROWS
CHIPS = 64
OWNERS = 16
PAY = 136
CONV = 4
LAG = CONV - 1

F32 = jnp.float32
BF16 = jnp.bfloat16


def dot(a, b, ca=1, cb=0):
    return lax.dot_general(a, b, (((ca,), (cb,)), ((), ())), preferred_element_type=F32)


def pack3(v):
    lane = lax.broadcasted_iota(jnp.int32, v.shape, 1)
    hi = v.astype(BF16).astype(F32)
    mid = (v - hi).astype(BF16).astype(F32)
    low = (v - hi - mid).astype(BF16).astype(F32)
    three = jnp.where(lane < 32, hi, jnp.where(lane < 64, pltpu.roll(mid, 32, 1), pltpu.roll(low, 64, 1)))
    return jnp.where(lane < 96, three, 0.0).astype(BF16)


def spread():
    row = lax.broadcasted_iota(jnp.int32, (128, WIDTH_X), 0)
    col = lax.broadcasted_iota(jnp.int32, (128, WIDTH_X), 1)
    return ((row & 31) == (col >> 6)).astype(F32).astype(BF16)


def table_kernel(conv_w, conv_b, gain, decay, skip, rows, table, rim):
    table[0:CONV] = 0.5 * conv_w[...].astype(F32)
    table[CONV : CONV + 1] = 0.5 * conv_b[...].astype(F32).reshape(1, GROUP_W)
    table[CONV + 1 : CONV + 2, 0:WIDTH_X] = gain[...].astype(F32).reshape(1, WIDTH_X)
    table[CONV + 1 : CONV + 2, WIDTH_X:] = jnp.zeros((1, GROUP_W - WIDTH_X), F32)
    table[CONV + 2 :] = jnp.zeros((8 - CONV - 2, GROUP_W), F32)
    d, s = decay[...].reshape(1, PER_GROUP), skip[...].reshape(1, PER_GROUP)
    table[CONV + 2 : CONV + 3, 0:256] = jnp.concatenate([d] * 4 + [s] * 4, 1)
    rim[...] = rows[...].astype(F32)[16 - LAG :].astype(BF16)


def first_kernel(ids, starts, mine, recv, rim_a, rim_b, dt_mine, dt_recv, tab0, tab1, tab2, tab3,
                 pay, act, xb, score, scale, tabs, ext, one_hot, afull, bfull, lrow, small, bnow):
    g = pl.program_id(0)
    core = ids[0]
    own = pl.multiple_of(core * ROWS, ROWS)
    other = pl.multiple_of((1 - core) * ROWS, ROWS)

    @pl.when(g == 0)
    def _():
        col = lax.broadcasted_iota(jnp.int32, (2 * 128, 128), 0)
        lane = lax.broadcasted_iota(jnp.int32, (2 * 128, 128), 1)
        pick = (col == ((2 * (lane >> 5) + core) << 5) + (lane & 31)).astype(F32).astype(BF16)
        afull[pl.ds(own, ROWS), :] = dot(dt_mine[...], pick)
        afull[pl.ds(other, ROWS), :] = dot(dt_recv[...], pick)
        step = jnp.log1p(jnp.exp(afull[...]))
        block = (lax.broadcasted_iota(jnp.int32, (1, 256), 1) >> 5) & 3
        every = jnp.zeros((1, 256), F32)
        for shift, tab in enumerate((tab0, tab1, tab2, tab3)):
            every = every + jnp.where(block == ((ids[1] - shift) & 3), tab[6:7, 0:256], 0.0)
        small[...] = every
        cum = -step * every[:, 0:128]
        row = lax.broadcasted_iota(jnp.int32, (CHUNK, 128), 0)
        shift = 1
        while shift < CHUNK:
            cum = cum + jnp.where(row >= shift, pltpu.roll(cum, shift, 0), 0.0)
            shift *= 2
        afull[...] = jnp.exp(cum)
        bfull[...] = jnp.exp(-cum) * step
        last = cum[CHUNK - 8 :, :]
        hi = last.astype(BF16).astype(F32)
        mid = (last - hi).astype(BF16).astype(F32)
        low = (last - hi - mid).astype(BF16).astype(F32)
        lrow[0:1] = hi[7:8]
        lrow[1:2] = mid[7:8]
        lrow[2:3] = low[7:8]
        lrow[3:8] = jnp.zeros((5, 128), F32)
        one_hot[...] = spread()

    shift = (ids[1] - g) & 3
    table = jnp.where(
        shift == 0, tab0[...], jnp.where(shift == 1, tab1[...], jnp.where(shift == 2, tab2[...], tab3[...]))
    )
    tabs[0] = table
    tabs[0, 7:8, 0:256] = small[...]

    back = (128 - g * PER_GROUP) & 127
    scale[0] = pack3(pltpu.roll(afull[...], back, 1))
    bnow[...] = pack3(pltpu.roll(bfull[...], back, 1))
    opens = starts[ids[2]] == ids[1] * CHUNK

    def conv(j):
        at = pl.ds(pl.multiple_of(j * 128, 128), 128)
        halo = rim_a[:, at].astype(F32) + rim_b[:, at].astype(F32)
        ext[j, 8 - LAG : 8, :] = jnp.where(opens, jnp.zeros_like(halo), halo)
        ext[j, pl.ds(8 + own, ROWS), :] = mine[:, at].astype(F32)
        ext[j, pl.ds(8 + other, ROWS), :] = recv[:, at].astype(F32)
        half = tabs[0, CONV : CONV + 1, at] + ext[j, 8 - LAG : 8 - LAG + CHUNK, :] * tabs[0, 0:1, at]
        for tap in range(1, CONV):
            half = half + ext[j, 8 - LAG + tap : 8 - LAG + tap + CHUNK, :] * tabs[0, tap : tap + 1, at]
        return at, (half * jnp.tanh(half) + half).astype(BF16)

    strips = WIDTH_X // 128
    _, b_in = conv(strips)
    _, c_out = conv(strips + 1)
    act[:, WIDTH_X : WIDTH_X + STATE] = b_in
    act[:, WIDTH_X + STATE :] = c_out
    b_t = b_in.astype(F32).T.astype(BF16)

    def weigh(j):
        at, val = conv(j)
        act[:, at] = val
        xb[:, at] = (val.astype(F32) * dot(bnow[...], one_hot[:, at])).astype(BF16)

    def fresh(j):
        at = pl.ds(pl.multiple_of(j * 128, 128), 128)
        pay[0, j, 0:STATE, :] = dot(b_t, xb[:, at]).astype(BF16)

    weigh(0)

    def strip(j, _):
        fresh(j - 1)
        weigh(j)
        return 0

    lax.fori_loop(1, strips, strip, 0)
    fresh(strips - 1)
    s = dot(c_out, b_in, 1, 1)
    t_at = lax.broadcasted_iota(jnp.int32, (CHUNK, CHUNK), 0)
    s_at = lax.broadcasted_iota(jnp.int32, (CHUNK, CHUNK), 1)
    score[...] = jnp.where(s_at <= t_at, s, 0.0).astype(BF16)
    for o in range(OWNERS):
        rows = []
        for slot in range(4):
            tap, block = divmod(o * 4 + slot, GROUP_W // 128)
            if tap < LAG:
                end = 8 + CHUNK - LAG + tap
                rows.append(ext[block, end : end + 1, :])
            else:
                rows.append(jnp.zeros((1, 128), F32))
        pay[0, o, STATE:PAY, :] = jnp.concatenate(rows + [lrow[0:4]], 0).astype(BF16)


def inner_kernel(score, xb, act, scale, tabs, part, one_hot):
    @pl.when(pl.program_id(0) == 0)
    def _():
        one_hot[...] = spread()

    back = (128 - pl.program_id(0) * PER_GROUP) & 127
    skip = pack3(pltpu.roll(jnp.broadcast_to(tabs[0, 7:8, 128:256], (8, 128)), back, 1))
    s = score[...]
    for j in range(0, WIDTH_X, 256):
        at = slice(j, j + 256)
        e = one_hot[:, at]
        part[:, at] = dot(scale[0], e) * dot(s, xb[:, at]) + dot(skip, e)[0:1] * act[:, at].astype(F32)


def scan_kernel(ids, starts, assign, got, held, fin, dec):
    lane = lax.broadcasted_iota(jnp.int32, (CHIPS, 128), 1)
    total = (got[:, STATE + 4, :].astype(F32) + got[:, STATE + 5, :].astype(F32)
             + got[:, STATE + 6, :].astype(F32))
    head = ids[1] * PER_GROUP + ids[2] * 2
    d0 = jnp.sum(jnp.where(lane == head, total, 0.0), 1, keepdims=True)
    d1 = jnp.sum(jnp.where(lane == head + 1, total, 0.0), 1, keepdims=True)
    dec[...] = jnp.exp(jnp.where(lane < HEAD_DIM, d0, d1))
    fin[...] = jnp.zeros_like(fin)

    def step(ctx, carry):
        state, count = carry
        for y in range(4):
            at = y * OWNERS + ctx
            opens = starts[ctx] == y * CHUNK
            state = jnp.where(opens, 0.0, state)
            count = count + opens.astype(jnp.int32)
            held[at] = state.astype(BF16)
            state = dec[pl.ds(at, 1), :] * (state + got[at, 0:STATE, :].astype(F32))
            if y < 3:
                ends = starts[ctx] == (y + 1) * CHUNK
            else:
                ends = (ctx == OWNERS - 1) | (starts[jnp.minimum(ctx + 1, OWNERS - 1)] == 0)

            @pl.when(ends)
            def _():
                to = assign[count - 1]
                fin[to, 0:STATE, :] = state.T.astype(BF16)
                fin[to, STATE:PAY, :] = got[at, STATE:PAY, :]

        return state, count

    lax.fori_loop(0, OWNERS, step, (jnp.zeros((STATE, 128), F32), jnp.int32(0)))


def last_kernel(ids, part, act_c, scale, held, tabs, out, y, one_hot):
    @pl.when(pl.program_id(0) == 0)
    def _():
        one_hot[...] = spread()

    c = act_c[...]
    square = jnp.zeros((ROWS, 128), F32)
    for o in range(0, OWNERS, 2):
        at = slice(o * 128, (o + 2) * 128)
        h = jnp.concatenate([held[0, o], held[0, o + 1]], 1)
        total = part[:, at] + dot(scale[0], one_hot[:, at]) * dot(c, h)
        y[:, at] = total
        square = square + total[:, :128] * total[:, :128] + total[:, 128:] * total[:, 128:]
    mean = jnp.sum(square, 1, keepdims=True) * (1.0 / WIDTH_X)
    inv = jnp.broadcast_to(lax.rsqrt(mean + 1e-05), (ROWS, 128))
    for j in range(0, WIDTH_X, 128):
        at = slice(j, j + 128)
        out[:, at] = (y[:, at] * inv * tabs[0, CONV + 1 : CONV + 2, at]).astype(BF16)


def place_kernel(ids, whole, theirs, out, held, sem_in, sem_out):
    def loads(g):
        cols = pl.ds(g * WIDTH_X, WIDTH_X)
        return pltpu.make_async_copy(theirs.at[:, cols], held.at[g], sem_in.at[g])

    def stores(g):
        cols = pl.ds(pl.multiple_of((2 * g + 1 - ids[0]) * WIDTH_X, WIDTH_X), WIDTH_X)
        return pltpu.make_async_copy(held.at[g], out.at[:, cols], sem_out.at[g])

    for g in range(LOC):
        loads(g).start()
    for g in range(LOC):
        loads(g).wait()
        stores(g).start()
    for g in range(LOC):
        stores(g).wait()


def rows_kernel(got, states, tails):
    states[...] = got[:, 0:STATE, :].astype(F32)
    for piece in range(LAG * GROUP_W // 128):
        tap, block = divmod(piece, GROUP_W // 128)
        row = STATE + piece % 4
        tails[0, tap : tap + 1, block * 128 : (block + 1) * 128] = got[piece // 4, row : row + 1, :]


FIRST, INNER, SCAN, LAST, PLACE, EXTRA, SMALL = 52, 52, 52, 52, 44, 52, 60


def params(grant, *semantics):
    return pltpu.CompilerParams(
        dimension_semantics=semantics or None, vmem_limit_bytes=grant * 2**20
    )


def wide(n):
    return pl.BlockSpec((CHUNK, n), lambda g, *_: (0, g))


TABLE = pl.BlockSpec((1, 8, GROUP_W), lambda g, *_: (g, 0, 0))


def last_call(ids, part, act, scale, held, tabs, own):
    half = (lambda ids: ids[0]) if own else (lambda ids: 1 - ids[0])
    cols = (lambda g, ids: 2 * g + ids[0]) if own else (lambda g, ids: g)
    width = (GROUPS if own else LOC) * WIDTH_X
    return pl.pallas_call(
        last_kernel,
        name="last",
        grid_spec=pltpu.PrefetchScalarGridSpec(
            num_scalar_prefetch=1,
            grid=(LOC,),
            in_specs=[
                pl.BlockSpec((ROWS, WIDTH_X), lambda g, ids: (half(ids), g)),
                pl.BlockSpec((ROWS, STATE), lambda g, ids: (half(ids), GROUP_W // 128 * (g + 1) - 1)),
                pl.BlockSpec((1, ROWS, 128), lambda g, ids: (g, half(ids), 0)),
                pl.BlockSpec((1, OWNERS, STATE, 128), lambda g, ids: (g, 0, 0, 0)),
                TABLE,
            ],
            out_specs=pl.BlockSpec((ROWS, WIDTH_X), lambda g, ids: (0, cols(g, ids))),
            scratch_shapes=[pltpu.VMEM((ROWS, WIDTH_X), F32), pltpu.VMEM((128, WIDTH_X), BF16)],
        ),
        out_shape=jax.ShapeDtypeStruct((ROWS, width), BF16),
        compiler_params=params(LAST, "arbitrary"),
        cost_estimate=pl.CostEstimate(flops=10**9, bytes_accessed=9 * 10**6, transcendentals=0),
    )(ids, part, act, scale, held, tabs)


def shards(xbc, dt_raw, decay_rate, skip, conv_w, conv_b, gain, starts, assign):
    core = lax.axis_index("core").astype(jnp.int32)
    y_at = lax.axis_index("y").astype(jnp.int32)
    ctx = (lax.axis_index("x") * 4 + lax.axis_index("z")).astype(jnp.int32)
    at = jnp.arange(4, dtype=jnp.int32)
    ids = jnp.where(at == 0, core, jnp.where(at == 1, y_at, ctx))

    swap = [(0, 1), (1, 0)]
    recv = lax.ppermute(xbc, "core", swap)
    dt_recv = lax.ppermute(dt_raw, "core", swap)

    full = lambda *shape: pl.BlockSpec(shape, lambda i: (0,) * len(shape))
    table, rim = pl.pallas_call(
        table_kernel,
        name="table",
        grid=(1,),
        in_specs=[
            full(CONV, GROUP_W),
            full(GROUP_W),
            full(WIDTH_X),
            full(PER_GROUP),
            full(PER_GROUP),
            pl.BlockSpec((16, GROUPS * GROUP_W), lambda i: (ROWS // 16 - 1, 0)),
        ],
        out_specs=[full(8, GROUP_W), full(LAG, GROUPS * GROUP_W)],
        out_shape=[
            jax.ShapeDtypeStruct((8, GROUP_W), F32),
            jax.ShapeDtypeStruct((LAG, GROUPS * GROUP_W), BF16),
        ],
        compiler_params=params(SMALL, "arbitrary"),
    )(conv_w, conv_b, gain, decay_rate, skip, xbc)
    names = ("x", "z", "y", "core")
    rims = [
        lax.ppermute(rim, names, [(2 * p + 1, 2 * p + 2 + k) for p in range(CHIPS - 1)])
        for k in range(2)
    ]
    tables = [table] + [
        lax.ppermute(table, "y", [(i, (i + s) % 4) for i in range(4)]) for s in range(1, 4)
    ]

    whole_table = pl.BlockSpec((8, GROUP_W), lambda g, *_: (0, 0))
    rows_spec = pl.BlockSpec((ROWS, GROUP_W), lambda g, ids, st: (0, 2 * g + ids[0]))
    rim_spec = pl.BlockSpec((LAG, GROUP_W), lambda g, ids, st: (0, 2 * g + ids[0]))
    dt_spec = pl.BlockSpec((ROWS, 256), lambda g, ids, st: (0, 0))
    scale_spec = pl.BlockSpec((1, CHUNK, 128), lambda g, *_: (g, 0, 0))

    pay, act, xb, score, scale, tabs = pl.pallas_call(
        first_kernel,
        name="first",
        grid_spec=pltpu.PrefetchScalarGridSpec(
            num_scalar_prefetch=2,
            grid=(LOC,),
            in_specs=[rows_spec] * 2 + [rim_spec] * 2 + [dt_spec] * 2 + [whole_table] * 4,
            out_specs=[
                pl.BlockSpec((1, OWNERS, PAY, 128), lambda g, *_: (g, 0, 0, 0)),
                wide(GROUP_W),
                wide(WIDTH_X),
                wide(CHUNK),
                scale_spec,
                TABLE,
            ],
            scratch_shapes=[
                pltpu.VMEM((GROUP_W // 128, 8 + CHUNK, 128), F32),
                pltpu.VMEM((128, WIDTH_X), BF16),
                pltpu.VMEM((CHUNK, 128), F32),
                pltpu.VMEM((CHUNK, 128), F32),
                pltpu.VMEM((8, 128), F32),
                pltpu.VMEM((1, 256), F32),
                pltpu.VMEM((CHUNK, 128), BF16),
            ],
        ),
        out_shape=[
            jax.ShapeDtypeStruct((LOC, OWNERS, PAY, 128), BF16),
            jax.ShapeDtypeStruct((CHUNK, LOC * GROUP_W), BF16),
            jax.ShapeDtypeStruct((CHUNK, LOC * WIDTH_X), BF16),
            jax.ShapeDtypeStruct((CHUNK, LOC * CHUNK), BF16),
            jax.ShapeDtypeStruct((LOC, CHUNK, 128), BF16),
            jax.ShapeDtypeStruct((LOC, 8, GROUP_W), F32),
        ],
        compiler_params=params(FIRST, "arbitrary"),
        cost_estimate=pl.CostEstimate(flops=2 * 10**9, bytes_accessed=18 * 10**6, transcendentals=0),
    )(ids, starts, xbc, recv, *rims, dt_raw, dt_recv, *tables)

    got = lax.all_to_all(pay.reshape(CHIPS, PAY, 128), ("y", "x", "z"), 0, 0, tiled=True)

    part = pl.pallas_call(
        inner_kernel,
        name="inner",
        grid=(LOC,),
        in_specs=[wide(CHUNK), wide(WIDTH_X), wide(GROUP_W), scale_spec, TABLE],
        out_specs=wide(WIDTH_X),
        out_shape=jax.ShapeDtypeStruct((CHUNK, LOC * WIDTH_X), F32),
        scratch_shapes=[pltpu.VMEM((128, WIDTH_X), BF16)],
        compiler_params=params(INNER, "arbitrary"),
        cost_estimate=pl.CostEstimate(flops=2 * 10**9, bytes_accessed=20 * 10**6, transcendentals=0),
    )(score, xb, act, scale, tabs)

    smem = pl.BlockSpec(memory_space=pltpu.SMEM)
    vmem = pl.BlockSpec(memory_space=pltpu.VMEM)
    held, fin = pl.pallas_call(
        scan_kernel,
        name="scan",
        in_specs=[smem, smem, smem, vmem],
        out_specs=[vmem, vmem],
        out_shape=[
            jax.ShapeDtypeStruct((CHIPS, STATE, 128), BF16),
            jax.ShapeDtypeStruct((OWNERS, PAY, 128), BF16),
        ],
        scratch_shapes=[pltpu.VMEM((CHIPS, 128), F32)],
        compiler_params=params(SCAN),
        cost_estimate=pl.CostEstimate(flops=10**7, bytes_accessed=5 * 10**6, transcendentals=0),
    )(ids, starts, assign, got)

    back = lax.all_to_all(held, ("y", "x", "z"), 0, 0, tiled=True)
    rows_got = lax.all_to_all(fin, ("x", "z"), 0, 0, tiled=True)

    back = back.reshape(LOC, OWNERS, STATE, 128)
    send = last_call(ids, part, act, scale, back, tabs, False)
    theirs = lax.ppermute(send, "core", swap)
    out = last_call(ids, part, act, scale, back, tabs, True)
    hbm = pl.BlockSpec(memory_space=pl.ANY)
    mixed = pl.pallas_call(
        place_kernel,
        name="place",
        in_specs=[smem, hbm, hbm],
        out_specs=hbm,
        out_shape=jax.ShapeDtypeStruct((ROWS, GROUPS * WIDTH_X), BF16),
        scratch_shapes=[
            pltpu.VMEM((LOC, ROWS, WIDTH_X), BF16),
            pltpu.SemaphoreType.DMA((LOC,)),
            pltpu.SemaphoreType.DMA((LOC,)),
        ],
        input_output_aliases={1: 0},
        compiler_params=params(PLACE),
    )(ids, out, theirs)
    states, tails = pl.pallas_call(
        rows_kernel,
        name="rows",
        in_specs=[vmem],
        out_specs=[vmem, vmem],
        out_shape=[
            jax.ShapeDtypeStruct((OWNERS, STATE, 128), F32),
            jax.ShapeDtypeStruct((1, LAG, GROUP_W), BF16),
        ],
        compiler_params=params(EXTRA),
    )(rows_got)
    return (mixed, states.reshape(1, PER_GROUP, HEAD_DIM, STATE), tails)


def solution(mesh):
    axes = ("x", "z", "y", "core")
    fine = Mesh(mesh.devices.reshape(4, 4, 4, 2), axes)
    head = ("y", "core")
    in_specs = (
        P(axes, None),
        P(axes, None),
        P(head),
        P(head),
        P(None, head),
        P(head),
        P(head),
        P(),
        P(),
    )
    out_specs = (P(axes, None), P(("x", "z"), head, None, None), P(("x", "z"), None, head))
    return jax.shard_map(shards, mesh=fine, in_specs=in_specs, out_specs=out_specs, check_vma=False)
```

```python
import functools

import jax
import jax.numpy as jnp
from jax import lax
from jax.experimental import pallas as pl
from jax.experimental.pallas import tpu as pltpu
from jax.sharding import Mesh, PartitionSpec as P


HEAD_DIM = 64
STATE = 128
GROUPS = 8
PER_GROUP = 32
WIDTH_X = PER_GROUP * HEAD_DIM
GROUP_W = WIDTH_X + 2 * STATE
LOC = GROUPS // 2
ROWS = 128
CHUNK = 2 * ROWS
CHIPS = 64
OWNERS = 16
PAY = 136
CONV = 4
LAG = CONV - 1

F32 = jnp.float32
BF16 = jnp.bfloat16


def dot(a, b, ca=1, cb=0):
    return lax.dot_general(a, b, (((ca,), (cb,)), ((), ())), preferred_element_type=F32)


def halves(v):
    hi = v.astype(BF16).astype(F32)
    return hi, (v - hi).astype(BF16).astype(F32)


def pack(hi, low, g):
    lane = lax.broadcasted_iota(jnp.int32, hi.shape, 1)
    both = jnp.where(
        lane < 32, pltpu.roll(hi, (128 - g * PER_GROUP) & 127, 1), pltpu.roll(low, (160 - g * PER_GROUP) & 127, 1)
    )
    return jnp.where(lane < 64, both, 0.0).astype(BF16)


def spread():
    row = lax.broadcasted_iota(jnp.int32, (128, WIDTH_X), 0)
    col = lax.broadcasted_iota(jnp.int32, (128, WIDTH_X), 1)
    return ((row & 31) == (col >> 6)).astype(F32).astype(BF16)


def table_kernel(conv_w, conv_b, gain, decay, skip, rows, table, rim):
    table[0:CONV] = 0.5 * conv_w[...].astype(F32)
    table[CONV : CONV + 1] = 0.5 * conv_b[...].astype(F32).reshape(1, GROUP_W)
    table[CONV + 1 : CONV + 2, 0:WIDTH_X] = gain[...].astype(F32).reshape(1, WIDTH_X)
    table[CONV + 1 : CONV + 2, WIDTH_X:] = jnp.zeros((1, GROUP_W - WIDTH_X), F32)
    table[CONV + 2 :] = jnp.zeros((8 - CONV - 2, GROUP_W), F32)
    d, s = decay[...].reshape(1, PER_GROUP), skip[...].reshape(1, PER_GROUP)
    table[CONV + 2 : CONV + 3, 0:256] = jnp.concatenate([d] * 4 + [s] * 4, 1)
    rim[...] = rows[...].astype(F32)[16 - LAG :].astype(BF16)


def first_kernel(ids, starts, mine, recv, rim_a, rim_b, dt_mine, dt_recv, tab0, tab1, tab2, tab3,
                 pay, act, scale, tabs, xb, ext_a, ext_b, one_hot, full, lrow, small, even, odd, ends):
    g = pl.program_id(0)
    core = ids[0]
    own = pl.multiple_of(core * ROWS, ROWS)
    other = pl.multiple_of((1 - core) * ROWS, ROWS)

    @pl.when(g == 0)
    def _():
        col = lax.broadcasted_iota(jnp.int32, (2 * 128, 128), 0)
        lane = lax.broadcasted_iota(jnp.int32, (2 * 128, 128), 1)
        pick = (col == ((2 * (lane >> 5) + core) << 5) + (lane & 31)).astype(F32).astype(BF16)
        full[0, pl.ds(own, ROWS), :] = dot(dt_mine[...], pick)
        full[0, pl.ds(other, ROWS), :] = dot(dt_recv[...], pick)
        step = jnp.log1p(jnp.exp(full[0]))
        block = (lax.broadcasted_iota(jnp.int32, (1, 256), 1) >> 5) & 3
        every = jnp.zeros((1, 256), F32)
        for shift, tab in enumerate((tab0, tab1, tab2, tab3)):
            every = every + jnp.where(block == ((ids[1] - shift) & 3), tab[6:7, 0:256], 0.0)
        small[...] = every
        cum = -step * every[:, 0:128]
        row = lax.broadcasted_iota(jnp.int32, (CHUNK, 128), 0)
        shift = 1
        while shift < CHUNK:
            cum = cum + jnp.where(row >= shift, pltpu.roll(cum, shift, 0), 0.0)
            shift *= 2
        full[0], full[1] = halves(jnp.exp(cum))
        full[2], full[3] = halves(jnp.exp(-cum) * step)
        last = cum[CHUNK - 8 :, :]
        hi, rest = halves(last)
        low = (last - hi - rest).astype(BF16).astype(F32)
        lrow[0:1] = hi[7:8]
        lrow[1:2] = rest[7:8]
        lrow[2:3] = low[7:8]
        lrow[3:8] = jnp.zeros((5, 128), F32)
        one_hot[...] = spread()

    shift = (ids[1] - g) & 3
    table = jnp.where(
        shift == 0, tab0[...], jnp.where(shift == 1, tab1[...], jnp.where(shift == 2, tab2[...], tab3[...]))
    )
    tabs[0] = table
    tabs[0, 7:8, 0:256] = small[...]
    scale[0, 0] = pack(full[0], full[1], g)
    scale[0, 1] = pack(full[2], full[3], g)
    opens = starts[ids[2]] == ids[1] * CHUNK

    def columns(j):
        return pl.ds(j * 128 if isinstance(j, int) else pl.multiple_of(j * 128, 128), 128)

    def conv(j, ext):
        at = columns(j)
        halo = rim_a[:, at].astype(F32) + rim_b[:, at].astype(F32)
        ext[8 - LAG : 8, :] = jnp.where(opens, jnp.zeros_like(halo), halo)
        ext[pl.ds(8 + own, ROWS), :] = mine[:, at].astype(F32)
        ext[pl.ds(8 + other, ROWS), :] = recv[:, at].astype(F32)
        half = tabs[0, CONV : CONV + 1, at] + ext[8 - LAG : 8 - LAG + CHUNK, :] * tabs[0, 0:1, at]
        for tap in range(1, CONV):
            half = half + ext[8 - LAG + tap : 8 - LAG + tap + CHUNK, :] * tabs[0, tap : tap + 1, at]
        ends[j] = ext[CHUNK : CHUNK + 8, :]
        val = (half * jnp.tanh(half) + half).astype(BF16)
        act[:, at] = val
        return val

    strips = WIDTH_X // 128
    b_in = conv(strips, ext_a)
    conv(strips + 1, ext_b)
    b_t = b_in.astype(F32).T.astype(BF16)

    def weights(j):
        return dot(scale[0, 1], one_hot[:, columns(j)])

    def fresh(j):
        pay[0, j, 0:STATE, :] = dot(b_t, xb[:, columns(j)]).astype(BF16)

    def weigh(j, ext, factor):
        xb[:, columns(j)] = (conv(j, ext).astype(F32) * factor[...]).astype(BF16)

    def pair(i, behind):
        if behind:
            fresh(2 * i - 2)
            fresh(2 * i - 1)
        odd[...] = weights(2 * i + 1)
        weigh(2 * i, ext_a, even)
        even[...] = weights((2 * i + 2) & (strips - 1))
        weigh(2 * i + 1, ext_b, odd)

    even[...] = weights(0)
    pair(0, False)

    def trip(i, _):
        pair(i, True)
        return 0

    lax.fori_loop(1, strips // 2, trip, 0)
    fresh(strips - 2)
    fresh(strips - 1)
    for o in range(OWNERS):
        rows = []
        for slot in range(4):
            tap, block = divmod(o * 4 + slot, GROUP_W // 128)
            if tap < LAG:
                rows.append(ends[block, 8 - LAG + tap : 9 - LAG + tap, :])
            else:
                rows.append(jnp.zeros((1, 128), F32))
        pay[0, o, STATE:PAY, :] = jnp.concatenate(rows + [lrow[0:4]], 0).astype(BF16)


def inner_kernel(act, scale, tabs, part, one_hot):
    g = pl.program_id(0)

    @pl.when(g == 0)
    def _():
        one_hot[...] = spread()

    skip_hi, rest = halves(jnp.broadcast_to(tabs[0, 7:8, 128:256], (8, 128)))
    skip = pack(skip_hi, rest, g)
    s = dot(act[:, WIDTH_X + STATE :], act[:, WIDTH_X : WIDTH_X + STATE], 1, 1)
    t_at = lax.broadcasted_iota(jnp.int32, (CHUNK, CHUNK), 0)
    s_at = lax.broadcasted_iota(jnp.int32, (CHUNK, CHUNK), 1)
    s = jnp.where(s_at <= t_at, s, 0.0).astype(BF16)
    for j in range(0, WIDTH_X, 256):
        at = slice(j, j + 256)
        e = one_hot[:, at]
        x = act[:, at].astype(F32)
        xb = (x * dot(scale[0, 1], e)).astype(BF16)
        part[:, at] = dot(scale[0, 0], e) * dot(s, xb) + dot(skip, e)[0:1] * x


def scan_kernel(ids, starts, assign, got, held, fin, dec, after):
    lane = lax.broadcasted_iota(jnp.int32, (CHIPS, 128), 1)
    total = (got[:, STATE + 4, :].astype(F32) + got[:, STATE + 5, :].astype(F32)
             + got[:, STATE + 6, :].astype(F32))
    head = ids[1] * PER_GROUP + ids[2] * 2
    d0 = jnp.sum(jnp.where(lane == head, total, 0.0), 1, keepdims=True)
    d1 = jnp.sum(jnp.where(lane == head + 1, total, 0.0), 1, keepdims=True)
    dec[...] = jnp.exp(jnp.where(lane < HEAD_DIM, d0, d1))
    fin[...] = jnp.zeros_like(fin)

    def step(ctx, state):
        for y in range(4):
            at = y * OWNERS + ctx
            if y % 2 == 0:
                state = jnp.where(starts[ctx] == y * CHUNK, 0.0, state)
            held[at] = state.astype(BF16)
            state = dec[pl.ds(at, 1), :] * (state + got[at, 0:STATE, :].astype(F32))
            if y % 2:
                after[2 * ctx + y // 2] = state
        return state

    lax.fori_loop(0, OWNERS, step, jnp.zeros((STATE, 128), F32))

    def close(i, count):
        ctx, second = i >> 1, i & 1
        count = count + (starts[ctx] == second * 2 * CHUNK).astype(jnp.int32)
        follow = starts[jnp.minimum(ctx + 1, OWNERS - 1)]
        ends = jnp.where(second == 1, (ctx == OWNERS - 1) | (follow == 0), starts[ctx] == 2 * CHUNK)

        @pl.when(ends)
        def _():
            to = assign[count - 1]
            fin[to, 0:STATE, :] = after[i].T.astype(BF16)
            fin[to, STATE:PAY, :] = got[(2 * second + 1) * OWNERS + ctx, STATE:PAY, :]

        return count

    lax.fori_loop(0, 2 * OWNERS, close, jnp.int32(0))


def last_kernel(row_at, col_at, ids, part, act, scale, held, tabs, out,
                y, one_hot, part_in, c_in, scale_in, held_in, tab_in, done, sem_in, sem_out):
    rows = pl.ds(pl.multiple_of(row_at(ids) * ROWS, ROWS), ROWS)
    loads = []
    for g in range(LOC):
        wide_cols = pl.ds(g * WIDTH_X, WIDTH_X)
        c_cols = pl.ds((g + 1) * GROUP_W - STATE, STATE)
        loads.append([
            pltpu.make_async_copy(held.at[g], held_in.at[g], sem_in.at[g, 0]),
            pltpu.make_async_copy(act.at[rows, c_cols], c_in.at[g], sem_in.at[g, 1]),
            pltpu.make_async_copy(scale.at[g, 0, rows], scale_in.at[g], sem_in.at[g, 2]),
            pltpu.make_async_copy(part.at[rows, wide_cols], part_in.at[g], sem_in.at[g, 3]),
            pltpu.make_async_copy(tabs.at[g], tab_in.at[g], sem_in.at[g, 4]),
        ])
    for group in loads:
        for copy in group:
            copy.start()
    one_hot[...] = spread()
    stores = []
    for g in range(LOC):
        for copy in loads[g]:
            copy.wait()
        c = c_in[g]
        square = jnp.zeros((ROWS, 128), F32)
        for o in range(0, OWNERS, 2):
            at = slice(o * 128, (o + 2) * 128)
            h = jnp.concatenate([held_in[g, o], held_in[g, o + 1]], 1)
            total = part_in[g, :, at] + dot(scale_in[g], one_hot[:, at]) * dot(c, h)
            y[:, at] = total
            square = square + total[:, :128] * total[:, :128] + total[:, 128:] * total[:, 128:]
        mean = jnp.sum(square, 1, keepdims=True) * (1.0 / WIDTH_X)
        inv = jnp.broadcast_to(lax.rsqrt(mean + 1e-05), (ROWS, 128))
        for j in range(0, WIDTH_X, 128):
            at = slice(j, j + 128)
            done[g, :, at] = (y[:, at] * inv * tab_in[g, CONV + 1 : CONV + 2, at]).astype(BF16)
        to = pl.ds(pl.multiple_of(col_at(g, ids) * WIDTH_X, WIDTH_X), WIDTH_X)
        stores.append(pltpu.make_async_copy(done.at[g], out.at[:, to], sem_out.at[g]))
        stores[g].start()
    for store in stores:
        store.wait()


def place_kernel(ids, whole, theirs, out, held, sem_in, sem_out):
    def loads(g):
        cols = pl.ds(g * WIDTH_X, WIDTH_X)
        return pltpu.make_async_copy(theirs.at[:, cols], held.at[g], sem_in.at[g])

    def stores(g):
        cols = pl.ds(pl.multiple_of((2 * g + 1 - ids[0]) * WIDTH_X, WIDTH_X), WIDTH_X)
        return pltpu.make_async_copy(held.at[g], out.at[:, cols], sem_out.at[g])

    for g in range(LOC):
        loads(g).start()
    for g in range(LOC):
        loads(g).wait()
        stores(g).start()
    for g in range(LOC):
        stores(g).wait()


def rows_kernel(got, states, tails):
    states[...] = got[:, 0:STATE, :].astype(F32)
    for piece in range(LAG * GROUP_W // 128):
        tap, block = divmod(piece, GROUP_W // 128)
        row = STATE + piece % 4
        tails[0, tap : tap + 1, block * 128 : (block + 1) * 128] = got[piece // 4, row : row + 1, :]


FIRST, INNER, SCAN, LAST, PLACE, EXTRA, SMALL = 52, 52, 40, 52, 44, 52, 60


def params(grant, *semantics):
    return pltpu.CompilerParams(
        dimension_semantics=semantics or None, vmem_limit_bytes=grant * 2**20
    )


def wide(n):
    return pl.BlockSpec((CHUNK, n), lambda g, *_: (0, g))


TABLE = pl.BlockSpec((1, 8, GROUP_W), lambda g, *_: (g, 0, 0))


SMEM = pl.BlockSpec(memory_space=pltpu.SMEM)
VMEM = pl.BlockSpec(memory_space=pltpu.VMEM)
HBM = pl.BlockSpec(memory_space=pl.ANY)


def last_call(ids, part, act, scale, held, tabs, own):
    row_at = (lambda ids: ids[0]) if own else (lambda ids: 1 - ids[0])
    col_at = (lambda g, ids: 2 * g + ids[0]) if own else (lambda g, ids: g)
    width = (GROUPS if own else LOC) * WIDTH_X
    return pl.pallas_call(
        functools.partial(last_kernel, row_at, col_at),
        name="last",
        in_specs=[SMEM] + [HBM] * 5,
        out_specs=HBM,
        out_shape=jax.ShapeDtypeStruct((ROWS, width), BF16),
        scratch_shapes=[
            pltpu.VMEM((ROWS, WIDTH_X), F32),
            pltpu.VMEM((128, WIDTH_X), BF16),
            pltpu.VMEM((LOC, ROWS, WIDTH_X), F32),
            pltpu.VMEM((LOC, ROWS, STATE), BF16),
            pltpu.VMEM((LOC, ROWS, 128), BF16),
            pltpu.VMEM((LOC, OWNERS, STATE, 128), BF16),
            pltpu.VMEM((LOC, 8, GROUP_W), F32),
            pltpu.VMEM((LOC, ROWS, WIDTH_X), BF16),
            pltpu.SemaphoreType.DMA((LOC, 5)),
            pltpu.SemaphoreType.DMA((LOC,)),
        ],
        compiler_params=params(LAST),
        cost_estimate=pl.CostEstimate(flops=10**9, bytes_accessed=9 * 10**6, transcendentals=0),
    )(ids, part, act, scale, held, tabs)


def shards(xbc, dt_raw, decay_rate, skip, conv_w, conv_b, gain, starts, assign):
    core = lax.axis_index("core").astype(jnp.int32)
    y_at = lax.axis_index("y").astype(jnp.int32)
    ctx = (lax.axis_index("x") * 4 + lax.axis_index("z")).astype(jnp.int32)
    at = jnp.arange(4, dtype=jnp.int32)
    ids = jnp.where(at == 0, core, jnp.where(at == 1, y_at, ctx))

    swap = [(0, 1), (1, 0)]
    recv = lax.ppermute(xbc, "core", swap)
    dt_recv = lax.ppermute(dt_raw, "core", swap)

    full = lambda *shape: pl.BlockSpec(shape, lambda i: (0,) * len(shape))
    table, rim = pl.pallas_call(
        table_kernel,
        name="table",
        grid=(1,),
        in_specs=[
            full(CONV, GROUP_W),
            full(GROUP_W),
            full(WIDTH_X),
            full(PER_GROUP),
            full(PER_GROUP),
            pl.BlockSpec((16, GROUPS * GROUP_W), lambda i: (ROWS // 16 - 1, 0)),
        ],
        out_specs=[full(8, GROUP_W), full(LAG, GROUPS * GROUP_W)],
        out_shape=[
            jax.ShapeDtypeStruct((8, GROUP_W), F32),
            jax.ShapeDtypeStruct((LAG, GROUPS * GROUP_W), BF16),
        ],
        compiler_params=params(SMALL, "arbitrary"),
    )(conv_w, conv_b, gain, decay_rate, skip, xbc)
    names = ("x", "z", "y", "core")
    rims = [
        lax.ppermute(rim, names, [(2 * p + 1, 2 * p + 2 + k) for p in range(CHIPS - 1)])
        for k in range(2)
    ]
    tables = [table] + [
        lax.ppermute(table, "y", [(i, (i + s) % 4) for i in range(4)]) for s in range(1, 4)
    ]

    whole_table = pl.BlockSpec((8, GROUP_W), lambda g, *_: (0, 0))
    rows_spec = pl.BlockSpec((ROWS, GROUP_W), lambda g, ids, st: (0, 2 * g + ids[0]))
    rim_spec = pl.BlockSpec((LAG, GROUP_W), lambda g, ids, st: (0, 2 * g + ids[0]))
    dt_spec = pl.BlockSpec((ROWS, 256), lambda g, ids, st: (0, 0))
    scale_spec = pl.BlockSpec((1, 2, CHUNK, 128), lambda g, *_: (g, 0, 0, 0))

    pay, act, scale, tabs = pl.pallas_call(
        first_kernel,
        name="first",
        grid_spec=pltpu.PrefetchScalarGridSpec(
            num_scalar_prefetch=2,
            grid=(LOC,),
            in_specs=[rows_spec] * 2 + [rim_spec] * 2 + [dt_spec] * 2 + [whole_table] * 4,
            out_specs=[
                pl.BlockSpec((1, OWNERS, PAY, 128), lambda g, *_: (g, 0, 0, 0)),
                wide(GROUP_W),
                scale_spec,
                TABLE,
            ],
            scratch_shapes=[
                pltpu.VMEM((CHUNK, WIDTH_X), BF16),
                pltpu.VMEM((8 + CHUNK, 128), F32),
                pltpu.VMEM((8 + CHUNK, 128), F32),
                pltpu.VMEM((128, WIDTH_X), BF16),
                pltpu.VMEM((4, CHUNK, 128), F32),
                pltpu.VMEM((8, 128), F32),
                pltpu.VMEM((1, 256), F32),
                pltpu.VMEM((CHUNK, 128), F32),
                pltpu.VMEM((CHUNK, 128), F32),
                pltpu.VMEM((GROUP_W // 128, 8, 128), F32),
            ],
        ),
        out_shape=[
            jax.ShapeDtypeStruct((LOC, OWNERS, PAY, 128), BF16),
            jax.ShapeDtypeStruct((CHUNK, LOC * GROUP_W), BF16),
            jax.ShapeDtypeStruct((LOC, 2, CHUNK, 128), BF16),
            jax.ShapeDtypeStruct((LOC, 8, GROUP_W), F32),
        ],
        compiler_params=params(FIRST, "arbitrary"),
        cost_estimate=pl.CostEstimate(flops=2 * 10**9, bytes_accessed=18 * 10**6, transcendentals=0),
    )(ids, starts, xbc, recv, *rims, dt_raw, dt_recv, *tables)

    got = lax.all_to_all(pay.reshape(CHIPS, PAY, 128), ("y", "x", "z"), 0, 0, tiled=True)

    part = pl.pallas_call(
        inner_kernel,
        name="inner",
        grid=(LOC,),
        in_specs=[wide(GROUP_W), scale_spec, TABLE],
        out_specs=wide(WIDTH_X),
        out_shape=jax.ShapeDtypeStruct((CHUNK, LOC * WIDTH_X), F32),
        scratch_shapes=[pltpu.VMEM((128, WIDTH_X), BF16)],
        compiler_params=params(INNER, "arbitrary"),
        cost_estimate=pl.CostEstimate(flops=2 * 10**9, bytes_accessed=20 * 10**6, transcendentals=0),
    )(act, scale, tabs)

    held, fin = pl.pallas_call(
        scan_kernel,
        name="scan",
        in_specs=[SMEM, SMEM, SMEM, VMEM],
        out_specs=[VMEM, VMEM],
        out_shape=[
            jax.ShapeDtypeStruct((CHIPS, STATE, 128), BF16),
            jax.ShapeDtypeStruct((OWNERS, PAY, 128), BF16),
        ],
        scratch_shapes=[pltpu.VMEM((CHIPS, 128), F32), pltpu.VMEM((2 * OWNERS, STATE, 128), F32)],
        compiler_params=params(SCAN),
        cost_estimate=pl.CostEstimate(flops=10**7, bytes_accessed=5 * 10**6, transcendentals=0),
    )(ids, starts, assign, got)

    back = lax.all_to_all(held, ("y", "x", "z"), 0, 0, tiled=True)
    rows_got = lax.all_to_all(fin, ("x", "z"), 0, 0, tiled=True)

    back = back.reshape(LOC, OWNERS, STATE, 128)
    send = last_call(ids, part, act, scale, back, tabs, False)
    theirs = lax.ppermute(send, "core", swap)
    out = last_call(ids, part, act, scale, back, tabs, True)
    mixed = pl.pallas_call(
        place_kernel,
        name="place",
        in_specs=[SMEM, HBM, HBM],
        out_specs=HBM,
        out_shape=jax.ShapeDtypeStruct((ROWS, GROUPS * WIDTH_X), BF16),
        scratch_shapes=[
            pltpu.VMEM((LOC, ROWS, WIDTH_X), BF16),
            pltpu.SemaphoreType.DMA((LOC,)),
            pltpu.SemaphoreType.DMA((LOC,)),
        ],
        input_output_aliases={1: 0},
        compiler_params=params(PLACE),
    )(ids, out, theirs)
    states, tails = pl.pallas_call(
        rows_kernel,
        name="rows",
        in_specs=[VMEM],
        out_specs=[VMEM, VMEM],
        out_shape=[
            jax.ShapeDtypeStruct((OWNERS, STATE, 128), F32),
            jax.ShapeDtypeStruct((1, LAG, GROUP_W), BF16),
        ],
        compiler_params=params(EXTRA),
    )(rows_got)
    return (mixed, states.reshape(1, PER_GROUP, HEAD_DIM, STATE), tails)


def solution(mesh):
    axes = ("x", "z", "y", "core")
    fine = Mesh(mesh.devices.reshape(4, 4, 4, 2), axes)
    head = ("y", "core")
    in_specs = (
        P(axes, None),
        P(axes, None),
        P(head),
        P(head),
        P(None, head),
        P(head),
        P(head),
        P(),
        P(),
    )
    out_specs = (P(axes, None), P(("x", "z"), head, None, None), P(("x", "z"), None, head))
    return jax.shard_map(shards, mesh=fine, in_specs=in_specs, out_specs=out_specs, check_vma=False)
```
